256 devices in a mesh: rows: 8 (over x, core), cols: 32 (over y, z).
Axes of the slice: x: 4, y: 4, z: 8, core: 2. Of those that a mesh axis runs over, the one named last changes fastest.
Arguments:
- image: bfloat16 [256, 256, 192], P('rows', 'cols'), may hold values from -6 to 6
- in_weight: bfloat16 [192, 768], replicated, may hold values from -0.4375 to 0.4375
- conv_weight: float32 [3, 3, 384], replicated, may hold values from -2 to 2
- conv_bias: float32 [384], replicated, may hold values from -3 to 3
- proj_weight: bfloat16 [4, 384, 44], replicated, may hold values from -0.3125 to 0.3125
- dt_weight: float32 [4, 12, 384], replicated, may hold values from -1.75 to 1.75
- dt_bias: float32 [4, 384], replicated, may hold values from -11 to -2.9
- a_log: float32 [4, 16, 384], replicated, may hold values from -0.7 to 2
- skip_gain: float32 [4, 384], replicated, may hold values from 0.05 to 0.5
- out_weight: bfloat16 [384, 192], replicated, may hold values from -0.3125 to 0.3125
Outputs:
- mixed: bfloat16 [256, 256, 192], P('rows', 'cols')
The draws below stay inside these ranges and needn't reach their ends.
All inputs are finite; a program needn't handle non-finite values.
Results may differ from the reference program's by a relative error of at most 0.012.
Values may be sent and summed in bfloat16 or wider, within the bound.
A program may use at most 192 MiB of HBM per device.

```python
import math
import jax
import jax.numpy as jnp
from jax import lax

DM = 192
INNER = 384
STATE = 16
RANK = 12
DIRS = 4
NH = 256
NW = 256


def draw_dt_bias(key, part):
    key_pick, key_slow, key_fast = jax.random.split(key, 3)
    share = 0.5
    picked = jax.random.uniform(key_pick, (DIRS, INNER)) < share
    chain_length = jnp.array([NW, NH, NW, NH], jnp.float32)[:, None]
    slow_step = jnp.exp(jax.random.uniform(key_slow, (DIRS, INNER), minval=jnp.log(0.1), maxval=jnp.log(0.5))) / chain_length
    fast_step = jnp.exp(jax.random.uniform(key_fast, (DIRS, INNER), minval=jnp.log(0.005), maxval=jnp.log(0.05)))
    chosen = jnp.where(picked, slow_step, fast_step)
    return jnp.log(jnp.expm1(chosen)).astype(jnp.float32)


def block_levels(key, extent, pieces, least, high):
    loudness, own = 1.0, jax.random.fold_in(key, 6)
    for axis_at, parts in pieces:
        draws = jnp.exp(jax.random.uniform(jax.random.fold_in(own, axis_at), (parts,), jnp.float32, least / len(pieces), high / len(pieces)))
        loudness = loudness * jnp.repeat(draws, extent[axis_at] // parts).reshape([-1 if axis == axis_at else 1 for axis in range(len(extent))])
    return loudness


def gaussian(own_key, extent, scale, limit, pieces=(), held_as=jnp.bfloat16):
    factor_of = block_levels(own_key, extent, pieces, -0.22, 0.18) if pieces else 1.0
    values = jax.random.normal(own_key, extent, jnp.float32) * scale * factor_of
    return jnp.minimum(jnp.maximum(values, -limit), limit).astype(held_as)


def setup_inputs(seed: int = 0) -> dict:
    keys = jax.random.split(jax.random.key(seed), 11)
    return {
        "image": gaussian(keys[0], (NH, NW, DM), 1.0, 6.0, ((0, 8), (1, 32))),
        "in_weight": gaussian(keys[1], (DM, 2 * INNER), DM ** -0.5, 0.4375),
        "conv_weight": gaussian(keys[2], (3, 3, INNER), 9 ** -0.5, 2.0, (), jnp.float32),
        "conv_bias": gaussian(keys[3], (INNER,), 0.5, 3.0, (), jnp.float32),
        "proj_weight": gaussian(keys[4], (DIRS, INNER, RANK + 2 * STATE), INNER ** -0.5, 0.3125),
        "dt_weight": gaussian(keys[5], (DIRS, RANK, INNER), RANK ** -0.5, 1.75, (), jnp.float32),
        "dt_bias": draw_dt_bias(jax.random.fold_in(keys[10], 71), 0),
        "a_log": jnp.clip(jax.random.uniform(keys[7], (DIRS, STATE, INNER), jnp.float32, -0.7, 2.0), -0.7, 2.0),
        "skip_gain": jnp.clip(jnp.exp(jax.random.uniform(keys[8], (DIRS, INNER), jnp.float32, math.log(0.05), math.log(0.5))), 0.05, 0.5),
        "out_weight": gaussian(keys[9], (INNER, DM), INNER ** -0.5, 0.3125),
    }


epsilon = 1e-05

def layer_norm(values):
    centre = values - lax.optimization_barrier(jnp.mean(values, axis=-1, keepdims=True))
    spread = lax.optimization_barrier(jnp.mean(centre * centre, axis=-1, keepdims=True))
    return centre * lax.rsqrt(spread + epsilon)

def sequence_scan(step_size, values, input_map, output_map, decay_rates):

    def advance(carry_state, inputs):
        part_step, part_values, part_in, part_out = inputs
        carry_state = jnp.exp(part_step[:, None, :] * decay_rates) * carry_state + (part_step * part_values)[:, None, :] * part_in[:, :, None]
        return (carry_state, jnp.einsum('qne,qn->qe', carry_state, part_out))
    zero_state = jnp.zeros((step_size.shape[1], decay_rates.shape[0], decay_rates.shape[1]), jnp.float32)
    _, outputs = lax.scan(advance, zero_state, (step_size, values, input_map, output_map))
    return outputs

def arrange(array, direction):
    if direction in (0, 2):
        array = jnp.swapaxes(array, 0, 1)
    if direction >= 2:
        array = jnp.flip(array, axis=0)
    return array

def restore(array, direction):
    if direction >= 2:
        array = jnp.flip(array, axis=0)
    if direction in (0, 2):
        array = jnp.swapaxes(array, 0, 1)
    return array

def reference(image, in_weight, conv_weight, conv_bias, proj_weight, dt_weight, dt_bias, a_log, skip_gain, out_weight):
    pixels = image.astype(jnp.float32)
    normed = layer_norm(pixels).astype(jnp.bfloat16).reshape(-1, DM)
    hidden = jnp.dot(normed, in_weight, preferred_element_type=jnp.float32)
    inner_act = hidden[:, :INNER].astype(jnp.bfloat16).reshape(NH, NW, INNER)
    gate_act = hidden[:, INNER:].astype(jnp.bfloat16).reshape(NH, NW, INNER)
    padded = jnp.pad(inner_act.astype(jnp.float32), ((1, 1), (1, 1), (0, 0)))
    conv_sum = jnp.zeros((NH, NW, INNER), jnp.float32)
    for row_shift in range(3):
        for col_shift in range(3):
            conv_sum = conv_sum + padded[row_shift:row_shift + NH, col_shift:col_shift + NW] * conv_weight[row_shift, col_shift]
    scanned = jax.nn.silu(conv_sum + conv_bias).astype(jnp.bfloat16)
    flat_values = scanned.reshape(-1, INNER)
    values = scanned.astype(jnp.float32)
    summed = jnp.zeros((NH, NW, INNER), jnp.float32)
    for direction in range(DIRS):
        projected = jnp.dot(flat_values, proj_weight[direction], preferred_element_type=jnp.float32)
        low_rank = projected[:, :RANK]
        input_map = projected[:, RANK:RANK + STATE].reshape(NH, NW, STATE)
        output_map = projected[:, RANK + STATE:].reshape(NH, NW, STATE)
        step_size = jax.nn.softplus(jnp.dot(low_rank, dt_weight[direction], precision=lax.Precision.HIGHEST, preferred_element_type=jnp.float32) + dt_bias[direction]).reshape(NH, NW, INNER)
        decay_rates = -jnp.exp(a_log[direction])
        result = sequence_scan(arrange(step_size, direction), arrange(values, direction), arrange(input_map, direction), arrange(output_map, direction), decay_rates)
        summed = summed + restore(result, direction) + skip_gain[direction] * values
    gated = (layer_norm(summed) * jax.nn.silu(gate_act.astype(jnp.float32))).astype(jnp.bfloat16)
    return jnp.dot(gated.reshape(-1, INNER), out_weight, preferred_element_type=jnp.float32).astype(jnp.bfloat16).reshape(NH, NW, DM)
```

```python
import functools
import math

import jax
import jax.numpy as jnp
from jax import lax
from jax.experimental import pallas as pl
from jax.experimental.pallas import tpu as pltpu
from jax.sharding import PartitionSpec as P

EPS = 1e-5
LOG2E = 1.0 / math.log(2.0)
MESH = pl.DeviceIdType.MESH
F32 = jnp.float32
BF16 = jnp.bfloat16
NR, NC = 8, 32
TR, TC = 32, 8
T = 256
E = 384
N = 16
RANK = 12
BL = 16
NB = T // BL


def norm_rows(v):
    centre = v - jnp.mean(v, axis=-1, keepdims=True)
    spread = jnp.mean(centre * centre, axis=-1, keepdims=True)
    return centre * lax.rsqrt(spread + EPS)


def silu(v):
    return v / (1.0 + jnp.exp(-v))


def softplus(v):
    return jnp.maximum(v, 0.0) + jnp.log1p(jnp.exp(-jnp.abs(v)))


def iota(shape, dim):
    return lax.broadcasted_iota(jnp.int32, shape, dim)


def kernel(
    img3, img2, win_h, cw_h, cb_h, proj_h, dtw_h, dtb_h, alog_h, skip_h, wout_h,
    out_ref,
    imgv, win, cw, cb, proj, dtw, dtb, alog, skip, wout,
    ecol, hal, xc, xl, xr, lh, rh, gate, tbuf, sval,
    sa, sc, rl, cl, rout, cout, rres, cres,
    linef, dts, us, bts, cms, hst, ys, tb2, imgf,
    wsem, hss, hrs, rss, rrs, css, crs, rss2, rrs2, css2, crs2,
):
    r = lax.axis_index("rows")
    c = lax.axis_index("cols")

    def col(k):
        return lax.rem(c + k + NC, NC)

    def row(k):
        return lax.rem(r + k + NR, NR)

    barrier = pltpu.get_barrier_semaphore()

    def hello(dr, dc):
        pl.semaphore_signal(barrier, inc=1, device_id=(dr, dc), device_id_type=MESH)

    def greet_cols(j, x):
        hello(r, col(j))
        return x

    def greet_rows(j, x):
        hello(row(j), c)
        return x

    lax.fori_loop(1, NC, greet_cols, 0)
    lax.fori_loop(1, NR, greet_rows, 0)
    for dr in (-1, 1):
        for dc in (-1, 1):
            hello(row(dr), col(dc))

    pairs = ((img2, imgv), (win_h, win), (cw_h, cw), (cb_h, cb), (proj_h, proj), (dtw_h, dtw),
             (dtb_h, dtb), (alog_h, alog), (skip_h, skip), (wout_h, wout))
    loads = [pltpu.make_async_copy(s, d, wsem.at[i]) for i, (s, d) in enumerate(pairs)]
    for load in loads:
        load.start()

    loads[0].wait()
    pixels = imgv[...].astype(F32)
    rest = pixels.shape[1] - 128
    imgf[0] = pixels[:, :128]
    imgf[1, :, pl.ds(0, rest)] = pixels[:, 128:]
    for side in (0, 1):
        at = pl.ds(side * (TC - 1), TR, stride=TC)
        edge = jnp.concatenate([imgf[0, at, :], imgf[1, at, :]], axis=1)[:, : 128 + rest]
        for k in range(4):
            ecol[side * 4 + k] = edge[k * 8 : (k + 1) * 8].astype(BF16)

    loads[1].wait()
    normed = norm_rows(pixels).astype(BF16)
    hidden = jnp.dot(normed, win[...], preferred_element_type=F32)
    xc[pl.ds(8, T), :] = hidden[:, :E].astype(BF16).astype(F32)
    gate[...] = silu(hidden[:, E:].astype(BF16).astype(F32))

    pl.semaphore_wait(barrier, (NC - 1) + (NR - 1) + 4)

    def halo(i, src, first, count, dr, dc):
        return pltpu.make_async_remote_copy(
            src_ref=src, dst_ref=hal.at[pl.ds(first, count)], send_sem=hss.at[i], recv_sem=hrs.at[i],
            device_id=(row(dr), col(dc)), device_id_type=MESH,
        )

    up, down = img3.at[pl.ds(0, 1)], img3.at[pl.ds(TR - 1, 1)]
    halos = [
        halo(0, ecol.at[pl.ds(4, 4)], 0, 4, 0, 1),
        halo(1, ecol.at[pl.ds(0, 4)], 4, 4, 0, -1),
        halo(2, down, 8, 1, 1, 0),
        halo(3, up, 9, 1, -1, 0),
        halo(4, down, 10, 1, 1, 1),
        halo(5, down, 11, 1, 1, -1),
        halo(6, up, 12, 1, -1, 1),
        halo(7, up, 13, 1, -1, -1),
    ]
    for copy in halos:
        copy.start()
    for copy in halos:
        copy.wait_recv()

    ring = jnp.concatenate([hal[k].astype(F32) for k in range(14)], axis=0)
    hin = jnp.dot(norm_rows(ring).astype(BF16), win[:, :E], preferred_element_type=F32)
    hin = hin.astype(BF16).astype(F32)
    has_l, has_r, has_u, has_d = c > 0, c < NC - 1, r > 0, r < NR - 1

    def kept(flag, v):
        return jnp.where(flag, v, jnp.zeros_like(v))

    lh[pl.ds(0, TR), :] = kept(has_l, hin[0:32])
    rh[pl.ds(0, TR), :] = kept(has_r, hin[32:64])
    xc[pl.ds(0, 8), :] = kept(has_u, hin[64:72])
    xc[pl.ds(8 + T, 8), :] = kept(has_d, hin[72:80])
    lh[pl.ds(32, 8), :] = kept(jnp.logical_and(has_u, has_l), hin[80:88])
    rh[pl.ds(32, 8), :] = kept(jnp.logical_and(has_u, has_r), hin[88:96])
    lh[pl.ds(40, 8), :] = kept(jnp.logical_and(has_d, has_l), hin[96:104])
    rh[pl.ds(40, 8), :] = kept(jnp.logical_and(has_d, has_r), hin[104:112])

    sub = iota((8, E), 0)

    def sides(q, lrow, rrow):
        at = pl.ds(pl.multiple_of(q * 8, 8), 8)
        v = xc[at, :]
        xl[at, :] = jnp.where(sub == 0, jnp.broadcast_to(lh[pl.ds(lrow, 1), :], (8, E)), pltpu.roll(v, 1, 0))
        xr[at, :] = jnp.where(sub == 7, jnp.broadcast_to(rh[pl.ds(rrow, 1), :], (8, E)), pltpu.roll(v, 7, 0))

    def all_sides(q, x):
        sides(q + 1, q, q)
        return x

    sides(0, 39, 32)
    sides(TR + 1, 47, 40)
    lax.fori_loop(0, TR, all_sides, 0, unroll=4)

    loads[2].wait()
    loads[3].wait()

    def conv(q, x):
        acc = jnp.broadcast_to(cb[...], (8, E))
        for i in range(3):
            at = pl.ds(pl.multiple_of((q + i) * 8, 8), 8)
            for j, ref in enumerate((xl, xc, xr)):
                acc = acc + ref[at, :] * cw[i, j : j + 1, :]
        s = silu(acc).astype(BF16)
        sa[q] = s
        sf = s.astype(F32)
        sval[pl.ds(pl.multiple_of(q * 8, 8), 8), :] = sf
        for k in range(3):
            tbuf[k, pl.ds(q, 8, stride=TR), :] = sf[:, k * 128 : (k + 1) * 128]
        return x

    lax.fori_loop(0, TR, conv, 0, unroll=2)
    for j in range(TC):
        for k in range(3):
            sc[j, :, pl.ds(k * 128, 128)] = tbuf[k, pl.ds(j * TR, TR), :].astype(BF16)

    def row_copy(d, slot, src, dst, ss, rs):
        return pltpu.make_async_remote_copy(
            src_ref=src.at[d], dst_ref=dst.at[slot], send_sem=ss.at[d], recv_sem=rs.at[slot],
            device_id=(r, d), device_id_type=MESH,
        )

    def col_copy(d, slot, src, dst, ss, rs):
        return pltpu.make_async_remote_copy(
            src_ref=src.at[d], dst_ref=dst.at[slot], send_sem=ss.at[d], recv_sem=rs.at[slot],
            device_id=(d, c), device_id_type=MESH,
        )

    def send(copy, turn, me, count, *refs):
        def one(j, x):
            copy(turn(j), me, *refs).start()
            return x

        lax.fori_loop(1, count, one, 0)

    def receive(copy, turn, me, count, *refs):
        def one(j, x):
            copy(turn(j), turn(j), *refs).wait_recv()
            return x

        lax.fori_loop(1, count, one, 0)

    def finish(copy, turn, me, count, *refs):
        def one(j, x):
            copy(turn(j), me, *refs).wait_send()
            return x

        lax.fori_loop(1, count, one, 0)

    row_out = (row_copy, col, c, NC, sa, rl, rss, rrs)
    col_out = (col_copy, row, r, NR, sc, cl, css, crs)
    row_back = (row_copy, col, c, NC, rout, rres, rss2, rrs2)
    col_back = (col_copy, row, r, NR, cout, cres, css2, crs2)

    send(*row_out)
    send(*col_out)
    rl[c] = sa[c]
    cl[r] = sc[r]
    for load in loads[4:]:
        load.wait()

    pick_b = (iota((N, 44), 1) == iota((N, 44), 0) + RANK).astype(BF16)
    pick_c = (iota((44, T), 0) == (iota((44, T), 1) & 15) + RANK + N).astype(BF16)
    diagonal = (iota((T, T), 0) & 15) == (iota((T, T), 1) >> 4)

    def scan_line(ks):
        rates = []
        xb = linef[...].astype(BF16)
        for d, k in enumerate(ks):
            p = jnp.dot(xb, proj[k], preferred_element_type=F32)
            low = jnp.dot(p[:, :RANK], dtw[k], precision=lax.Precision.HIGHEST, preferred_element_type=F32)
            dt = softplus(low + dtb[k : k + 1, :])
            dts[d] = dt
            us[d] = dt * linef[...]
            pb = p.astype(BF16)
            bt = lax.dot_general(pick_b, pb, (((1,), (1,)), ((), ())), preferred_element_type=F32)
            for b in range(NB):
                bts[d, b] = bt[:, b * BL : (b + 1) * BL]
            ct = jnp.dot(pb, pick_c, preferred_element_type=F32)
            cms[d] = jnp.where(diagonal, ct, 0.0).astype(BF16)
            rates.append(jnp.exp(alog[k]) * (-LOG2E))

        def block(i, carry):
            h = list(carry)
            bs = (i, NB - 1 - i)
            base = [pl.multiple_of(b * BL, BL) for b in bs]
            maps = [bts[d, bs[d]] for d in (0, 1)]
            for step in range(BL):
                for d in (0, 1):
                    u = step if d == 0 else BL - 1 - step
                    dt = jnp.broadcast_to(dts[d, pl.ds(base[d] + u, 1), :], (8, E))
                    ux = jnp.broadcast_to(us[d, pl.ds(base[d] + u, 1), :], (8, E))
                    for half in (0, 1):
                        at = slice(half * 8, half * 8 + 8)
                        decay = jnp.exp2(dt * rates[d][at])
                        h[2 * d + half] = decay * h[2 * d + half] + ux * maps[d][at, u : u + 1]
                    both = jnp.concatenate([h[2 * d], h[2 * d + 1]], axis=0)
                    hst[d, u * N : (u + 1) * N, :] = both.astype(BF16)
            for d in (0, 1):
                ys[d, pl.ds(base[d], BL), :] = jnp.dot(
                    cms[d, pl.ds(base[d], BL), :], hst[d], preferred_element_type=F32
                )
            return tuple(h)

        zero = jnp.zeros((8, E), F32)
        lax.fori_loop(0, NB, block, (zero,) * 4)

    receive(*col_out)
    for j in range(NR):
        linef[pl.ds(j * TR, TR), :] = cl[j].astype(F32)
    scan_line((1, 3))
    for j in range(NR):
        at = pl.ds(j * TR, TR)
        cout[j] = (ys[0, at, :] + ys[1, at, :]).astype(BF16)
    send(*col_back)
    cres[r] = cout[r]

    receive(*row_out)
    for j in range(NC):
        linef[pl.ds(j * TC, TC), :] = rl[j].astype(F32)
    scan_line((0, 2))
    for j in range(NC):
        at = pl.ds(j * TC, TC)
        rout[j] = (ys[0, at, :] + ys[1, at, :]).astype(BF16)
    send(*row_back)
    rres[c] = rout[c]

    direct = skip[0:1, :] + skip[1:2, :] + skip[2:3, :] + skip[3:4, :]
    receive(*col_back)
    for j in range(TC):
        for k in range(3):
            tb2[k, pl.ds(j * TR, TR), :] = cres[j, :, pl.ds(k * 128, 128)].astype(F32)
    receive(*row_back)

    def total(q, x):
        at = pl.ds(pl.multiple_of(q * 8, 8), 8)
        parts = [tb2[k, pl.ds(q, 8, stride=TR), :] for k in range(3)]
        s = jnp.concatenate(parts, axis=1) + rres[q].astype(F32) + direct * sval[at, :]
        ys[0, at, :] = s
        return x

    lax.fori_loop(0, TR, total, 0, unroll=4)
    gated = (norm_rows(ys[0]) * gate[...]).astype(BF16)
    out_ref[...] = jnp.dot(gated, wout[...], preferred_element_type=F32).astype(BF16)

    for copy in halos:
        copy.wait_send()
    finish(*row_out)
    finish(*col_out)
    finish(*row_back)
    finish(*col_back)


def step(image, in_weight, conv_weight, conv_bias, proj_weight, dt_weight, dt_bias, a_log, skip_gain, out_weight):
    channels = image.shape[2]
    anywhere = pl.BlockSpec(memory_space=pl.ANY)
    vmem = pltpu.VMEM
    dma = pltpu.SemaphoreType.DMA
    bias = conv_bias.reshape(1, E)
    flat = image.reshape(T, channels)
    args = (image, flat, in_weight, conv_weight, bias, proj_weight, dt_weight, dt_bias, a_log, skip_gain, out_weight)
    result = pl.pallas_call(
        kernel,
        out_shape=jax.ShapeDtypeStruct((T, channels), BF16),
        in_specs=[anywhere] * len(args),
        out_specs=pl.BlockSpec(memory_space=pltpu.VMEM),
        scratch_shapes=[vmem(a.shape, a.dtype) for a in args[1:]]
        + [
            vmem((8, 8, channels), BF16),
            vmem((14, 8, channels), BF16),
            vmem((T + 16, E), F32),
            vmem((T + 16, E), F32),
            vmem((T + 16, E), F32),
            vmem((48, E), F32),
            vmem((48, E), F32),
            vmem((T, E), F32),
            vmem((3, T, 128), F32),
            vmem((T, E), F32),
            vmem((TR, TC, E), BF16),
            vmem((TC, TR, E), BF16),
            vmem((NC, TC, E), BF16),
            vmem((NR, TR, E), BF16),
            vmem((NC, TC, E), BF16),
            vmem((NR, TR, E), BF16),
            vmem((NC, TC, E), BF16),
            vmem((NR, TR, E), BF16),
            vmem((T, E), F32),
            vmem((2, T, E), F32),
            vmem((2, T, E), F32),
            vmem((2, NB, N, BL), F32),
            vmem((2, T, T), BF16),
            vmem((2, T, E), BF16),
            vmem((2, T, E), F32),
            vmem((3, T, 128), F32),
            vmem((2, T, 128), F32),
            dma((10,)), dma((8,)), dma((8,)),
            dma((NC,)), dma((NC,)), dma((NR,)), dma((NR,)),
            dma((NC,)), dma((NC,)), dma((NR,)), dma((NR,)),
        ],
        compiler_params=pltpu.CompilerParams(
            collective_id=0, has_side_effects=True, vmem_limit_bytes=48 * 1024 * 1024
        ),
    )(*args)
    return result.reshape(image.shape)


def solution(mesh):
    return jax.shard_map(
        step,
        mesh=mesh,
        in_specs=(P("rows", "cols", None), P(), P(), P(), P(), P(), P(), P(), P(), P()),
        out_specs=P("rows", "cols", None),
        check_vma=False,
    )
```

```python
import functools
import math

import jax
import jax.numpy as jnp
from jax import lax
from jax.experimental import pallas as pl
from jax.experimental.pallas import tpu as pltpu
from jax.sharding import PartitionSpec as P

EPS = 1e-5
LOG2E = 1.0 / math.log(2.0)
MESH = pl.DeviceIdType.MESH
F32 = jnp.float32
BF16 = jnp.bfloat16
NR, NC = 8, 32
TR, TC = 32, 8
T = 256
E = 384
N = 16
RANK = 12
BL = 16
NB = T // BL


def norm_rows(v):
    centre = v - jnp.mean(v, axis=-1, keepdims=True)
    spread = jnp.mean(centre * centre, axis=-1, keepdims=True)
    return centre * lax.rsqrt(spread + EPS)


def silu(v):
    w = 0.5 * v
    return w + w * jnp.tanh(w)


def softplus(v):
    return jnp.maximum(v, 0.0) + jnp.log1p(jnp.exp(-jnp.abs(v)))


def iota(shape, dim):
    return lax.broadcasted_iota(jnp.int32, shape, dim)


def kernel(
    img3, img2, win_h, cw_h, cb_h, proj_h, dtw_h, dtb_h, alog_h, skip_h, wout_h,
    out_ref,
    imgv, win, cw, cb, proj, dtw, dtb, alog, skip, wout,
    ecol, hal, xc, xl, xr, lh, rh, gate, tbuf, sval,
    sa, sc, rl, cl, rout, cout, rres, cres,
    linef, dts, us, rts, bts, cms, hst, ys, tb2, imgf, tot,
    wsem, hss, hrs, rss, rrs, css, crs, rss2, rrs2, css2, crs2,
):
    r = lax.axis_index("rows")
    c = lax.axis_index("cols")

    def col(k):
        return lax.rem(c + k + NC, NC)

    def row(k):
        return lax.rem(r + k + NR, NR)

    barrier = pltpu.get_barrier_semaphore()

    def hello(dr, dc):
        pl.semaphore_signal(barrier, inc=1, device_id=(dr, dc), device_id_type=MESH)

    def greet_cols(j, x):
        hello(r, col(j))
        return x

    def greet_rows(j, x):
        hello(row(j), c)
        return x

    lax.fori_loop(1, NC, greet_cols, 0)
    lax.fori_loop(1, NR, greet_rows, 0)
    for dr in (-1, 1):
        for dc in (-1, 1):
            hello(row(dr), col(dc))

    pairs = ((img2, imgv), (win_h, win), (cw_h, cw), (cb_h, cb), (proj_h, proj), (dtw_h, dtw),
             (dtb_h, dtb), (alog_h, alog), (skip_h, skip), (wout_h, wout))
    loads = [pltpu.make_async_copy(s, d, wsem.at[i]) for i, (s, d) in enumerate(pairs)]
    for load in loads:
        load.start()

    loads[0].wait()
    pixels = imgv[...].astype(F32)
    rest = pixels.shape[1] - 128
    imgf[0] = pixels[:, :128]
    imgf[1, :, pl.ds(0, rest)] = pixels[:, 128:]
    for side in (0, 1):
        at = pl.ds(side * (TC - 1), TR, stride=TC)
        edge = jnp.concatenate([imgf[0, at, :], imgf[1, at, :]], axis=1)[:, : 128 + rest]
        for k in range(4):
            ecol[side * 4 + k] = edge[k * 8 : (k + 1) * 8].astype(BF16)

    loads[1].wait()
    normed = norm_rows(pixels).astype(BF16)
    hidden = jnp.dot(normed, win[...], preferred_element_type=F32)
    xc[pl.ds(8, T), :] = hidden[:, :E].astype(BF16).astype(F32)
    gate[...] = silu(hidden[:, E:].astype(BF16).astype(F32))

    pl.semaphore_wait(barrier, (NC - 1) + (NR - 1) + 4)

    def halo(i, src, first, count, dr, dc):
        return pltpu.make_async_remote_copy(
            src_ref=src, dst_ref=hal.at[pl.ds(first, count)], send_sem=hss.at[i], recv_sem=hrs.at[i],
            device_id=(row(dr), col(dc)), device_id_type=MESH,
        )

    up, down = img3.at[pl.ds(0, 1)], img3.at[pl.ds(TR - 1, 1)]
    halos = [
        halo(0, ecol.at[pl.ds(4, 4)], 0, 4, 0, 1),
        halo(1, ecol.at[pl.ds(0, 4)], 4, 4, 0, -1),
        halo(2, down, 8, 1, 1, 0),
        halo(3, up, 9, 1, -1, 0),
        halo(4, down, 10, 1, 1, 1),
        halo(5, down, 11, 1, 1, -1),
        halo(6, up, 12, 1, -1, 1),
        halo(7, up, 13, 1, -1, -1),
    ]
    for copy in halos:
        copy.start()
    for copy in halos:
        copy.wait_recv()

    ring = jnp.concatenate([hal[k].astype(F32) for k in range(14)], axis=0)
    hin = jnp.dot(norm_rows(ring).astype(BF16), win[:, :E], preferred_element_type=F32)
    hin = hin.astype(BF16).astype(F32)
    has_l, has_r, has_u, has_d = c > 0, c < NC - 1, r > 0, r < NR - 1

    def kept(flag, v):
        return jnp.where(flag, v, jnp.zeros_like(v))

    lh[pl.ds(0, TR), :] = kept(has_l, hin[0:32])
    rh[pl.ds(0, TR), :] = kept(has_r, hin[32:64])
    xc[pl.ds(0, 8), :] = kept(has_u, hin[64:72])
    xc[pl.ds(8 + T, 8), :] = kept(has_d, hin[72:80])
    lh[pl.ds(32, 8), :] = kept(jnp.logical_and(has_u, has_l), hin[80:88])
    rh[pl.ds(32, 8), :] = kept(jnp.logical_and(has_u, has_r), hin[88:96])
    lh[pl.ds(40, 8), :] = kept(jnp.logical_and(has_d, has_l), hin[96:104])
    rh[pl.ds(40, 8), :] = kept(jnp.logical_and(has_d, has_r), hin[104:112])

    sub = iota((8, E), 0)

    def sides(q, lrow, rrow):
        at = pl.ds(pl.multiple_of(q * 8, 8), 8)
        v = xc[at, :]
        xl[at, :] = jnp.where(sub == 0, jnp.broadcast_to(lh[pl.ds(lrow, 1), :], (8, E)), pltpu.roll(v, 1, 0))
        xr[at, :] = jnp.where(sub == 7, jnp.broadcast_to(rh[pl.ds(rrow, 1), :], (8, E)), pltpu.roll(v, 7, 0))

    def all_sides(q, x):
        sides(q + 1, q, q)
        return x

    sides(0, 39, 32)
    sides(TR + 1, 47, 40)
    lax.fori_loop(0, TR, all_sides, 0, unroll=4)

    loads[2].wait()
    loads[3].wait()

    def conv(q, x):
        acc = jnp.broadcast_to(cb[...].reshape(1, E), (8, E))
        for i in range(3):
            at = pl.ds(pl.multiple_of((q + i) * 8, 8), 8)
            for j, ref in enumerate((xl, xc, xr)):
                acc = acc + ref[at, :] * cw[i, j : j + 1, :]
        s = silu(acc).astype(BF16)
        sa[q] = s
        sf = s.astype(F32)
        sval[pl.ds(pl.multiple_of(q * 8, 8), 8), :] = sf
        for k in range(3):
            tbuf[k, pl.ds(q, 8, stride=TR), :] = sf[:, k * 128 : (k + 1) * 128]
        return x

    lax.fori_loop(0, TR, conv, 0, unroll=4)
    for j in range(TC):
        for k in range(3):
            sc[j, :, pl.ds(k * 128, 128)] = tbuf[k, pl.ds(j * TR, TR), :].astype(BF16)

    def row_copy(d, slot, src, dst, ss, rs):
        return pltpu.make_async_remote_copy(
            src_ref=src.at[d], dst_ref=dst.at[slot], send_sem=ss.at[d], recv_sem=rs.at[slot],
            device_id=(r, d), device_id_type=MESH,
        )

    def col_copy(d, slot, src, dst, ss, rs):
        return pltpu.make_async_remote_copy(
            src_ref=src.at[d], dst_ref=dst.at[slot], send_sem=ss.at[d], recv_sem=rs.at[slot],
            device_id=(d, c), device_id_type=MESH,
        )

    def send(copy, turn, me, count, *refs):
        def one(j, x):
            copy(turn(j), me, *refs).start()
            return x

        lax.fori_loop(1, count, one, 0)

    def receive(copy, turn, me, count, *refs):
        def one(j, x):
            copy(turn(j), turn(j), *refs).wait_recv()
            return x

        lax.fori_loop(1, count, one, 0)

    def finish(copy, turn, me, count, *refs):
        def one(j, x):
            copy(turn(j), me, *refs).wait_send()
            return x

        lax.fori_loop(1, count, one, 0)

    row_out = (row_copy, col, c, NC, sa, rl, rss, rrs)
    col_out = (col_copy, row, r, NR, sc, cl, css, crs)
    row_back = (row_copy, col, c, NC, rout, rres, rss2, rrs2)
    col_back = (col_copy, row, r, NR, cout, cres, css2, crs2)

    send(*row_out)
    send(*col_out)
    rl[c] = sa[c]
    cl[r] = sc[r]
    for load in loads[4:]:
        load.wait()

    pick_b = (iota((N, 44), 1) == iota((N, 44), 0) + RANK).astype(BF16)
    pick_c = (iota((44, T), 0) == (iota((44, T), 1) & 15) + RANK + N).astype(BF16)
    diagonal = (iota((T, T), 0) & 15) == (iota((T, T), 1) >> 4)

    def scan_line(ks):
        xb = linef[...].astype(BF16)
        for d, k in enumerate(ks):
            wk = proj[:, k, :].astype(BF16)
            p = lax.dot_general(xb, wk, (((1,), (1,)), ((), ())), preferred_element_type=F32)
            pb = p.astype(BF16)
            rest = (p - pb.astype(F32)).astype(BF16)
            w = dtw[:, k, :]
            wb = w.astype(BF16)
            wrest = (w - wb.astype(F32)).astype(BF16)
            low = jnp.dot(pb[:, :RANK], wb, preferred_element_type=F32)
            low = low + jnp.dot(rest[:, :RANK], wb, preferred_element_type=F32)
            low = low + jnp.dot(pb[:, :RANK], wrest, preferred_element_type=F32)
            dt = softplus(low + dtb[k : k + 1, :])
            dts[d] = dt
            us[d] = dt * linef[...]
            bt = lax.dot_general(pick_b, pb, (((1,), (1,)), ((), ())), preferred_element_type=F32)
            for b in range(NB):
                bts[d, b] = bt[:, b * BL : (b + 1) * BL]
            ct = jnp.dot(pb, pick_c, preferred_element_type=F32)
            cms[d] = jnp.where(diagonal, ct, 0.0).astype(BF16)
            rts[d] = jnp.exp(alog[k]) * (-LOG2E)

        def readout(slot, bs):
            for d in (0, 1):
                b = bs[d]
                rows = pl.ds(pl.multiple_of(b * BL, BL), BL)
                maps = cms[d, rows, :]
                ys[d, pl.ds(pl.multiple_of((b + 1) * BL, BL), BL), :] = jnp.dot(
                    maps, hst[d, slot], preferred_element_type=F32
                )

        def block(bs, slot, h):
            base = [pl.multiple_of(b * BL, BL) for b in bs]
            maps = [bts[d, bs[d]] for d in (0, 1)]
            for step in range(BL):
                for d in (0, 1):
                    u = step if d == 0 else BL - 1 - step
                    dt = jnp.broadcast_to(dts[d, pl.ds(base[d] + u, 1), :], (8, E))
                    ux = jnp.broadcast_to(us[d, pl.ds(base[d] + u, 1), :], (8, E))
                    for half in (0, 1):
                        at = slice(half * 8, half * 8 + 8)
                        decay = jnp.exp2(dt * rts[d, at, :])
                        h[2 * d + half] = decay * h[2 * d + half] + ux * maps[d][at, u : u + 1]
                    both = jnp.concatenate([h[2 * d], h[2 * d + 1]], axis=0)
                    hst[d, slot, u * N : (u + 1) * N, :] = both.astype(BF16)

        def pair(i, carry):
            h = list(carry)
            b = 2 * i

            @pl.when(i > 0)
            def _():
                readout(1, (b - 1, NB - b))

            block((b, NB - 1 - b), 0, h)
            readout(0, (b, NB - 1 - b))
            block((b + 1, NB - 2 - b), 1, h)
            return tuple(h)

        zero = jnp.zeros((8, E), F32)
        lax.fori_loop(0, NB // 2, pair, (zero,) * 4)
        readout(1, (NB - 1, 0))

    receive(*col_out)
    for j in range(NR):
        linef[pl.ds(j * TR, TR), :] = cl[j].astype(F32)
    scan_line((1, 3))
    for j in range(NR):
        at = pl.ds(BL + j * TR, TR)
        cout[j] = (ys[0, at, :] + ys[1, at, :]).astype(BF16)
    send(*col_back)
    cres[r] = cout[r]

    receive(*row_out)
    for j in range(NC):
        linef[pl.ds(j * TC, TC), :] = rl[j].astype(F32)
    scan_line((0, 2))
    for j in range(NC):
        at = pl.ds(BL + j * TC, TC)
        rout[j] = (ys[0, at, :] + ys[1, at, :]).astype(BF16)
    send(*row_back)
    rres[c] = rout[c]

    direct = skip[0:1, :] + skip[1:2, :] + skip[2:3, :] + skip[3:4, :]
    receive(*col_back)
    for j in range(TC):
        for k in range(3):
            tb2[k, pl.ds(j * TR, TR), :] = cres[j, :, pl.ds(k * 128, 128)].astype(F32)
    receive(*row_back)

    def total(q, x):
        at = pl.ds(pl.multiple_of(q * 8, 8), 8)
        parts = [tb2[k, pl.ds(q, 8, stride=TR), :] for k in range(3)]
        s = jnp.concatenate(parts, axis=1) + rres[q].astype(F32) + direct * sval[at, :]
        tot[at, :] = s
        return x

    lax.fori_loop(0, TR, total, 0, unroll=4)
    gated = (norm_rows(tot[...]) * gate[...]).astype(BF16)
    mixed = lax.dot_general(gated, wout[...], (((1,), (1,)), ((), ())), preferred_element_type=F32)
    out_ref[...] = mixed.astype(BF16)

    for copy in halos:
        copy.wait_send()
    finish(*row_out)
    finish(*col_out)
    finish(*row_back)
    finish(*col_back)


def step(image, in_weight, conv_weight, conv_bias, proj_weight, dt_weight, dt_bias, a_log, skip_gain, out_weight):
    channels = image.shape[2]
    anywhere = pl.BlockSpec(memory_space=pl.ANY)
    vmem = pltpu.VMEM
    dma = pltpu.SemaphoreType.DMA
    flat = image.reshape(T, channels)
    maps = jnp.transpose(proj_weight, (2, 0, 1))
    low = jnp.transpose(dt_weight, (1, 0, 2))
    back = jnp.transpose(out_weight, (1, 0))
    args = (image, flat, in_weight, conv_weight, conv_bias, maps, low, dt_bias, a_log, skip_gain, back)
    result = pl.pallas_call(
        kernel,
        out_shape=jax.ShapeDtypeStruct((T, channels), BF16),
        in_specs=[anywhere] * len(args),
        out_specs=pl.BlockSpec(memory_space=pltpu.VMEM),
        scratch_shapes=[vmem(a.shape, a.dtype) for a in args[1:]]
        + [
            vmem((8, 8, channels), BF16),
            vmem((14, 8, channels), BF16),
            vmem((T + 16, E), F32),
            vmem((T + 16, E), F32),
            vmem((T + 16, E), F32),
            vmem((48, E), F32),
            vmem((48, E), F32),
            vmem((T, E), F32),
            vmem((3, T, 128), F32),
            vmem((T, E), F32),
            vmem((TR, TC, E), BF16),
            vmem((TC, TR, E), BF16),
            vmem((NC, TC, E), BF16),
            vmem((NR, TR, E), BF16),
            vmem((NC, TC, E), BF16),
            vmem((NR, TR, E), BF16),
            vmem((NC, TC, E), BF16),
            vmem((NR, TR, E), BF16),
            vmem((T, E), F32),
            vmem((2, T, E), F32),
            vmem((2, T, E), F32),
            vmem((2, N, E), F32),
            vmem((2, NB, N, BL), F32),
            vmem((2, T, T), BF16),
            vmem((2, 2, T, E), BF16),
            vmem((2, T + 2 * BL, E), F32),
            vmem((3, T, 128), F32),
            vmem((2, T, 128), F32),
            vmem((T, E), F32),
            dma((10,)), dma((8,)), dma((8,)),
            dma((NC,)), dma((NC,)), dma((NR,)), dma((NR,)),
            dma((NC,)), dma((NC,)), dma((NR,)), dma((NR,)),
        ],
        compiler_params=pltpu.CompilerParams(
            collective_id=0, has_side_effects=True, vmem_limit_bytes=62 * 1024 * 1024
        ),
    )(*args)
    return result.reshape(image.shape)


def solution(mesh):
    return jax.shard_map(
        step,
        mesh=mesh,
        in_specs=(P("rows", "cols", None), P(), P(), P(), P(), P(), P(), P(), P(), P()),
        out_specs=P("rows", "cols", None),
        check_vma=False,
    )
```

```python
import functools
import math

import jax
import jax.numpy as jnp
from jax import lax
from jax.experimental import pallas as pl
from jax.experimental.pallas import tpu as pltpu
from jax.sharding import PartitionSpec as P

EPS = 1e-5
LOG2E = 1.0 / math.log(2.0)
MESH = pl.DeviceIdType.MESH
F32 = jnp.float32
BF16 = jnp.bfloat16
NR, NC = 8, 32
TR, TC = 32, 8
T = 256
E = 384
N = 16
RANK = 12
KP = 3 * RANK + 2 * N
BL = 16
NB = T // BL


def norm_rows(v):
    centre = v - jnp.mean(v, axis=-1, keepdims=True)
    spread = jnp.mean(centre * centre, axis=-1, keepdims=True)
    return centre * lax.rsqrt(spread + EPS)


def silu(v):
    w = 0.5 * v
    return w + w * jnp.tanh(w)


def softplus(v):
    return jnp.maximum(v, 0.0) + jnp.log1p(jnp.exp(-jnp.abs(v)))


def iota(shape, dim):
    return lax.broadcasted_iota(jnp.int32, shape, dim)


def kernel(
    img3, img2, win_h, cw_h, cb_h, proj_h, dtw_h, dtb_h, alog_h, skip_h, wout_h,
    out_ref,
    imgv, win, cw, cb, proj, dtw, dtb, alog, skip, wout,
    ecol, hal, xc, xl, xr, lh, rh, gate, tbuf, sval,
    sa, sc, rl, cl, rout, cout, rres, cres,
    linef, dts, us, rts, wf, tf, wks, wds, bts, cms, hst, ys, tb2, imgf, tot,
    wsem, hss, hrs, rss, rrs, css, crs, rss2, rrs2, css2, crs2,
):
    r = lax.axis_index("rows")
    c = lax.axis_index("cols")

    def col(k):
        return lax.rem(c + k + NC, NC)

    def row(k):
        return lax.rem(r + k + NR, NR)

    barrier = pltpu.get_barrier_semaphore()

    def hello(dr, dc):
        pl.semaphore_signal(barrier, inc=1, device_id=(dr, dc), device_id_type=MESH)

    def greet_cols(j, x):
        hello(r, col(j))
        return x

    def greet_rows(j, x):
        hello(row(j), c)
        return x

    lax.fori_loop(1, NC, greet_cols, 0)
    lax.fori_loop(1, NR, greet_rows, 0)
    for dr in (-1, 1):
        for dc in (-1, 1):
            hello(row(dr), col(dc))

    pairs = ((img2, imgv), (win_h, win), (cw_h, cw), (cb_h, cb), (proj_h, proj), (dtw_h, dtw),
             (dtb_h, dtb), (alog_h, alog), (skip_h, skip), (wout_h, wout))
    loads = [pltpu.make_async_copy(s, d, wsem.at[i]) for i, (s, d) in enumerate(pairs)]
    for load in loads:
        load.start()

    loads[0].wait()
    pixels = imgv[...].astype(F32)
    rest = pixels.shape[1] - 128
    imgf[0] = pixels[:, :128]
    imgf[1, :, pl.ds(0, rest)] = pixels[:, 128:]
    for side in (0, 1):
        at = pl.ds(side * (TC - 1), TR, stride=TC)
        edge = jnp.concatenate([imgf[0, at, :], imgf[1, at, :]], axis=1)[:, : 128 + rest]
        for k in range(4):
            ecol[side * 4 + k] = edge[k * 8 : (k + 1) * 8].astype(BF16)

    pl.semaphore_wait(barrier, (NC - 1) + (NR - 1) + 4)

    def halo(i, src, first, count, dr, dc):
        return pltpu.make_async_remote_copy(
            src_ref=src, dst_ref=hal.at[pl.ds(first, count)], send_sem=hss.at[i], recv_sem=hrs.at[i],
            device_id=(row(dr), col(dc)), device_id_type=MESH,
        )

    up, down = img3.at[pl.ds(0, 1)], img3.at[pl.ds(TR - 1, 1)]
    halos = [
        halo(0, ecol.at[pl.ds(4, 4)], 0, 4, 0, 1),
        halo(1, ecol.at[pl.ds(0, 4)], 4, 4, 0, -1),
        halo(2, down, 8, 1, 1, 0),
        halo(3, up, 9, 1, -1, 0),
        halo(4, down, 10, 1, 1, 1),
        halo(5, down, 11, 1, 1, -1),
        halo(6, up, 12, 1, -1, 1),
        halo(7, up, 13, 1, -1, -1),
    ]
    for copy in halos:
        copy.start()

    loads[1].wait()
    normed = norm_rows(pixels).astype(BF16)
    hidden = jnp.dot(normed, win[...], preferred_element_type=F32)
    xc[pl.ds(8, T), :] = hidden[:, :E].astype(BF16).astype(F32)
    gate[...] = silu(hidden[:, E:].astype(BF16).astype(F32))


    for load in (loads[4], loads[5], loads[7]):
        load.wait()
    for k in range(4):
        wide = proj[:, k, :].astype(F32)
        for copy in range(3):
            wf[k, copy * RANK : (copy + 1) * RANK, :] = wide[:RANK]
        wf[k, 3 * RANK : 3 * RANK + 2 * N, :] = wide[RANK:]
        wks[k] = wf[k].astype(BF16)
        w = dtw[:, k, :]
        top = w.astype(BF16).astype(F32)
        tf[k, 0:RANK, :] = top
        tf[k, RANK : 2 * RANK, :] = top
        tf[k, 2 * RANK : 3 * RANK, :] = w - top
        wds[k] = tf[k].astype(BF16)
        rts[k] = jnp.exp(alog[k]) * (-LOG2E)

    for copy in halos:
        copy.wait_recv()

    ring = jnp.concatenate([hal[k].astype(F32) for k in range(14)], axis=0)
    hin = jnp.dot(norm_rows(ring).astype(BF16), win[:, :E], preferred_element_type=F32)
    hin = hin.astype(BF16).astype(F32)
    has_l, has_r, has_u, has_d = c > 0, c < NC - 1, r > 0, r < NR - 1

    def kept(flag, v):
        return jnp.where(flag, v, jnp.zeros_like(v))

    lh[pl.ds(0, TR), :] = kept(has_l, hin[0:32])
    rh[pl.ds(0, TR), :] = kept(has_r, hin[32:64])
    xc[pl.ds(0, 8), :] = kept(has_u, hin[64:72])
    xc[pl.ds(8 + T, 8), :] = kept(has_d, hin[72:80])
    lh[pl.ds(32, 8), :] = kept(jnp.logical_and(has_u, has_l), hin[80:88])
    rh[pl.ds(32, 8), :] = kept(jnp.logical_and(has_u, has_r), hin[88:96])
    lh[pl.ds(40, 8), :] = kept(jnp.logical_and(has_d, has_l), hin[96:104])
    rh[pl.ds(40, 8), :] = kept(jnp.logical_and(has_d, has_r), hin[104:112])

    sub = iota((8, E), 0)

    def sides(q, lrow, rrow):
        at = pl.ds(pl.multiple_of(q * 8, 8), 8)
        v = xc[at, :]
        xl[at, :] = jnp.where(sub == 0, jnp.broadcast_to(lh[pl.ds(lrow, 1), :], (8, E)), pltpu.roll(v, 1, 0))
        xr[at, :] = jnp.where(sub == 7, jnp.broadcast_to(rh[pl.ds(rrow, 1), :], (8, E)), pltpu.roll(v, 7, 0))

    def all_sides(q, x):
        sides(q + 1, q, q)
        return x

    sides(0, 39, 32)
    sides(TR + 1, 47, 40)
    lax.fori_loop(0, TR, all_sides, 0, unroll=4)

    loads[2].wait()
    loads[3].wait()

    def conv(q, x):
        acc = jnp.broadcast_to(cb[...].reshape(1, E), (8, E))
        for i in range(3):
            at = pl.ds(pl.multiple_of((q + i) * 8, 8), 8)
            for j, ref in enumerate((xl, xc, xr)):
                acc = acc + ref[at, :] * cw[i, j : j + 1, :]
        s = silu(acc).astype(BF16)
        sa[q] = s
        sf = s.astype(F32)
        sval[pl.ds(pl.multiple_of(q * 8, 8), 8), :] = sf
        for k in range(3):
            tbuf[k, pl.ds(q, 8, stride=TR), :] = sf[:, k * 128 : (k + 1) * 128]
        return x

    lax.fori_loop(0, TR, conv, 0, unroll=4)
    for j in range(TC):
        for k in range(3):
            sc[j, :, pl.ds(k * 128, 128)] = tbuf[k, pl.ds(j * TR, TR), :].astype(BF16)

    def row_copy(d, slot, src, dst, ss, rs):
        return pltpu.make_async_remote_copy(
            src_ref=src.at[d], dst_ref=dst.at[slot], send_sem=ss.at[d], recv_sem=rs.at[slot],
            device_id=(r, d), device_id_type=MESH,
        )

    def col_copy(d, slot, src, dst, ss, rs):
        return pltpu.make_async_remote_copy(
            src_ref=src.at[d], dst_ref=dst.at[slot], send_sem=ss.at[d], recv_sem=rs.at[slot],
            device_id=(d, c), device_id_type=MESH,
        )

    def send(copy, turn, me, count, *refs):
        def one(j, x):
            copy(turn(j), me, *refs).start()
            return x

        lax.fori_loop(1, count, one, 0)

    def receive(copy, turn, me, count, *refs):
        def one(j, x):
            copy(turn(j), turn(j), *refs).wait_recv()
            return x

        lax.fori_loop(1, count, one, 0)

    def finish(copy, turn, me, count, *refs):
        def one(j, x):
            copy(turn(j), me, *refs).wait_send()
            return x

        lax.fori_loop(1, count, one, 0)

    row_out = (row_copy, col, c, NC, sa, rl, rss, rrs)
    col_out = (col_copy, row, r, NR, sc, cl, css, crs)
    row_back = (row_copy, col, c, NC, rout, rres, rss2, rrs2)
    col_back = (col_copy, row, r, NR, cout, cres, css2, crs2)

    send(*col_out)
    send(*row_out)
    rl[c] = sa[c]
    cl[r] = sc[r]
    for load in (loads[6], loads[8], loads[9]):
        load.wait()

    pick_b = (iota((N, KP), 1) == iota((N, KP), 0) + 3 * RANK).astype(BF16)
    pick_c = (iota((KP, T), 0) == (iota((KP, T), 1) & 15) + 3 * RANK + N).astype(BF16)
    diagonal = (iota((BL, T), 0) == (iota((BL, T), 1) >> 4)).astype(F32)
    lane = iota((T, KP), 1)
    middle = jnp.logical_and(lane >= RANK, lane < 2 * RANK)

    def scan_line(ks, ready):
        xb = linef[...].astype(BF16)
        for d, k in enumerate(ks):
            p = lax.dot_general(xb, wks[k], (((1,), (1,)), ((), ())), preferred_element_type=F32)
            pb = p.astype(BF16)
            parts = jnp.where(middle, p - pb.astype(F32), p).astype(BF16)
            low = jnp.dot(parts[:, : 3 * RANK], wds[k], preferred_element_type=F32)
            dt = softplus(low + dtb[k : k + 1, :])
            dts[d] = dt
            us[d] = dt * linef[...]
            bt = lax.dot_general(pick_b, pb, (((1,), (1,)), ((), ())), preferred_element_type=F32)
            for b in range(NB):
                bts[d, b] = bt[:, b * BL : (b + 1) * BL]
            ct = jnp.dot(pb, pick_c, preferred_element_type=F32)
            cms[d] = (ct.reshape(NB, BL, T) * diagonal[None]).reshape(T, T).astype(BF16)

        def readout(slot, bs):
            for d in (0, 1):
                b = bs[d]
                rows = pl.ds(pl.multiple_of(jnp.clip(b, 0, NB - 1) * BL, BL), BL)
                maps = cms[d, rows, :]
                ys[d, pl.ds(pl.multiple_of((b + 1) * BL, BL), BL), :] = jnp.dot(
                    maps, hst[d, slot], preferred_element_type=F32
                )

        def block(bs, slot, h):
            base = [pl.multiple_of(b * BL, BL) for b in bs]
            maps = [bts[d, bs[d]] for d in (0, 1)]
            for step in range(BL):
                for d in (0, 1):
                    u = step if d == 0 else BL - 1 - step
                    dt = jnp.broadcast_to(dts[d, pl.ds(base[d] + u, 1), :], (8, E))
                    ux = jnp.broadcast_to(us[d, pl.ds(base[d] + u, 1), :], (8, E))
                    for half in (0, 1):
                        at = slice(half * 8, half * 8 + 8)
                        decay = jnp.exp2(dt * rts[ks[d], at, :])
                        h[2 * d + half] = decay * h[2 * d + half] + ux * maps[d][at, u : u + 1]
                    both = jnp.concatenate([h[2 * d], h[2 * d + 1]], axis=0)
                    hst[d, slot, u * N : (u + 1) * N, :] = both.astype(BF16)

        def pair(i, carry):
            h = list(carry)
            b = 2 * i

            ready(b)
            readout(1, (b - 1, NB - b))
            block((b, NB - 1 - b), 0, h)
            readout(0, (b, NB - 1 - b))
            block((b + 1, NB - 2 - b), 1, h)
            return tuple(h)

        zero = jnp.zeros((8, E), F32)
        for d in (0, 1):
            hst[d, 1] = jnp.zeros((T, E), BF16)
        lax.fori_loop(0, NB // 2, pair, (zero,) * 4)
        readout(1, (NB - 1, 0))

    receive(*col_out)
    for j in range(NR):
        linef[pl.ds(j * TR, TR), :] = cl[j].astype(F32)
    scan_line((1, 3), lambda b: None)
    for j in range(NR):
        at = pl.ds(BL + j * TR, TR)
        cout[j] = (ys[0, at, :] + ys[1, at, :]).astype(BF16)
    send(*col_back)
    cres[r] = cout[r]

    receive(*row_out)
    for j in range(NC):
        linef[pl.ds(j * TC, TC), :] = rl[j].astype(F32)

    def emit(x):
        for part in range(2):
            j = 2 * x + part
            at = pl.ds(pl.multiple_of(BL + j * TC, TC), TC)
            rout[j] = (ys[0, at, :] + ys[1, at, :]).astype(BF16)

            @pl.when(j != c)
            def _():
                row_copy(j, c, rout, rres, rss2, rrs2).start()

    def ready(b):
        @pl.when(b > NB // 2)
        def _():
            emit(b - 2)
            emit(NB + 1 - b)

        @pl.when(b > NB // 2 + 2)
        def _():
            emit(b - 3)
            emit(NB + 2 - b)

    scan_line((0, 2), ready)
    for x in (0, 15, 1, 14, 2, 13):
        emit(x)
    rres[c] = rout[c]

    direct = skip[0:1, :] + skip[1:2, :] + skip[2:3, :] + skip[3:4, :]
    receive(*col_back)
    for j in range(TC):
        for k in range(3):
            tb2[k, pl.ds(j * TR, TR), :] = cres[j, :, pl.ds(k * 128, 128)].astype(F32)

    def local(q, x):
        at = pl.ds(pl.multiple_of(q * 8, 8), 8)
        parts = [tb2[k, pl.ds(q, 8, stride=TR), :] for k in range(3)]
        tot[at, :] = jnp.concatenate(parts, axis=1) + direct * sval[at, :]
        return x

    lax.fori_loop(0, TR, local, 0, unroll=4)
    receive(*row_back)
    for q in range(TR):
        at = pl.ds(q * 8, 8)
        tot[at, :] = tot[at, :] + rres[q].astype(F32)
    gated = (norm_rows(tot[...]) * gate[...]).astype(BF16)
    mixed = lax.dot_general(gated, wout[...], (((1,), (1,)), ((), ())), preferred_element_type=F32)
    out_ref[...] = mixed.astype(BF16)

    for copy in halos:
        copy.wait_send()
    finish(*row_out)
    finish(*col_out)
    finish(*row_back)
    finish(*col_back)


def step(image, in_weight, conv_weight, conv_bias, proj_weight, dt_weight, dt_bias, a_log, skip_gain, out_weight):
    channels = image.shape[2]
    anywhere = pl.BlockSpec(memory_space=pl.ANY)
    vmem = pltpu.VMEM
    dma = pltpu.SemaphoreType.DMA
    flat = image.reshape(T, channels)
    maps = jnp.transpose(proj_weight, (2, 0, 1))
    low = jnp.transpose(dt_weight, (1, 0, 2))
    back = jnp.transpose(out_weight, (1, 0))
    args = (image, flat, in_weight, conv_weight, conv_bias, maps, low, dt_bias, a_log, skip_gain, back)
    result = pl.pallas_call(
        kernel,
        out_shape=jax.ShapeDtypeStruct((T, channels), BF16),
        in_specs=[anywhere] * len(args),
        out_specs=pl.BlockSpec(memory_space=pltpu.VMEM),
        scratch_shapes=[vmem(a.shape, a.dtype) for a in args[1:]]
        + [
            vmem((8, 8, channels), BF16),
            vmem((14, 8, channels), BF16),
            vmem((T + 16, E), F32),
            vmem((T + 16, E), F32),
            vmem((T + 16, E), F32),
            vmem((48, E), F32),
            vmem((48, E), F32),
            vmem((T, E), F32),
            vmem((3, T, 128), F32),
            vmem((T, E), F32),
            vmem((TR, TC, E), BF16),
            vmem((TC, TR, E), BF16),
            vmem((NC, TC, E), BF16),
            vmem((NR, TR, E), BF16),
            vmem((NC, TC, E), BF16),
            vmem((NR, TR, E), BF16),
            vmem((NC, TC, E), BF16),
            vmem((NR, TR, E), BF16),
            vmem((T, E), F32),
            vmem((2, T, E), F32),
            vmem((2, T, E), F32),
            vmem((4, N, E), F32),
            vmem((4, KP, E), F32),
            vmem((4, 3 * RANK, E), F32),
            vmem((4, KP, E), BF16),
            vmem((4, 3 * RANK, E), BF16),
            vmem((2, NB, N, BL), F32),
            vmem((2, T, T), BF16),
            vmem((2, 2, T, E), BF16),
            vmem((2, T + 2 * BL, E), F32),
            vmem((3, T, 128), F32),
            vmem((2, T, 128), F32),
            vmem((T, E), F32),
            dma((10,)), dma((8,)), dma((8,)),
            dma((NC,)), dma((NC,)), dma((NR,)), dma((NR,)),
            dma((NC,)), dma((NC,)), dma((NR,)), dma((NR,)),
        ],
        compiler_params=pltpu.CompilerParams(
            collective_id=0, has_side_effects=True, vmem_limit_bytes=62 * 1024 * 1024
        ),
    )(*args)
    return result.reshape(image.shape)


def solution(mesh):
    return jax.shard_map(
        step,
        mesh=mesh,
        in_specs=(P("rows", "cols", None), P(), P(), P(), P(), P(), P(), P(), P(), P()),
        out_specs=P("rows", "cols", None),
        check_vma=False,
    )
```
